256 devices in a mesh: batch: 64 (over y, z, x_hi), mp: 4 (over x_lo, core).
Axes of the slice: x: 4 (x_hi: 2, x_lo: 2; x = x_hi * 2 + x_lo), y: 4, z: 8, core: 2. Of those that a mesh axis runs over, the one named last changes fastest.
Arguments:
- img_feat: bfloat16 [131072, 768], P(('batch', 'mp')), may hold values from -6 to 6
- txt_feat: bfloat16 [131072, 768], P(('batch', 'mp')), may hold values from -6 to 6
- img_proj: bfloat16 [768, 768], P('mp'), may hold values from -0.21875 to 0.21875
- txt_proj: bfloat16 [768, 768], P('mp'), may hold values from -0.21875 to 0.21875
- logit_scale: float32 [], replicated, may hold values from 2 to 3
- bias: float32 [], replicated, may hold values from -2 to 0
Outputs:
- mean_loss: float32 [], replicated
- grad_logit_scale: float32 [], replicated
- grad_bias: float32 [], replicated
- grad_img_proj: float32 [768, 768], P('mp')
- grad_txt_proj: float32 [768, 768], P('mp')
The draws below stay inside these ranges and needn't reach their ends.
All inputs are finite; a program needn't handle non-finite values.
Results may differ from the reference program's by a relative error of at most 0.0008.
Values may be sent and summed in bfloat16 or wider, within the bound.
A program may use at most 128 MiB of HBM per device.

```python
import jax
import jax.numpy as jnp
from jax import lax

E = 768
D = 768
ROWS = 512
GROUP = 8
IMAGES = 131072
N_BATCH = 64
N_MP = 4


def levels(stream_key, extent, pieces, least, high):
    factor_of, own = 1.0, jax.random.fold_in(stream_key, 6)
    for position, parts in pieces:
        heights = jnp.exp(jax.random.uniform(jax.random.fold_in(own, position), (parts,), jnp.float32, least / len(pieces), high / len(pieces)))
        factor_of = factor_of * jnp.repeat(heights, extent[position] // parts).reshape([-1 if axis == position else 1 for axis in range(len(extent))])
    return factor_of


def normal_values(own_key, dims, deviation, most, pieces=(), dtype=jnp.bfloat16):
    entries = deviation * jax.random.normal(own_key, dims, jnp.float32)
    if pieces:
        entries = entries * levels(own_key, dims, pieces, -0.22, 0.18)
    return jnp.clip(entries, -most, most).astype(dtype)


def setup_inputs(seed: int = 0) -> dict:
    keys = jax.random.split(jax.random.key(seed), 7)
    img_feat = normal_values(keys[0], (IMAGES, E), 1.0, 6.0, ((0, 256),))
    txt_feat = normal_values(keys[1], (IMAGES, E), 1.0, 6.0, ((0, 256),))
    img_proj = normal_values(keys[2], (E, D), E ** -0.5, 0.21875, ((0, 4),))
    txt_proj = normal_values(keys[3], (E, D), E ** -0.5, 0.21875, ((0, 4),))
    logit_scale = jnp.clip(jax.random.uniform(keys[4], (), jnp.float32, 2.0, 3.0), 2.0, 3.0)
    bias = jnp.clip(jax.random.uniform(keys[5], (), jnp.float32, -2.0, 0.0), -2.0, 0.0)
    return {"img_feat": img_feat, "txt_feat": txt_feat, "img_proj": img_proj, "txt_proj": txt_proj, "logit_scale": logit_scale, "bias": bias}


def normalize(u):
    r = lax.rsqrt(lax.optimization_barrier(jnp.sum(u * u, axis=1, keepdims=True)) + 1e-06)
    zf = u * r
    return (zf, r, zf.astype(jnp.bfloat16))

def regroup(z):
    z = z.reshape(N_BATCH // GROUP, GROUP, N_MP, ROWS, z.shape[-1])
    z = jnp.transpose(z, (0, 2, 1, 3, 4))
    return z.reshape(N_BATCH // GROUP * N_MP, GROUP * ROWS, z.shape[-1])

def ungroup(z):
    z = z.reshape(N_BATCH // GROUP, N_MP, GROUP, ROWS, z.shape[-1])
    z = jnp.transpose(z, (0, 2, 1, 3, 4))
    return z.reshape(IMAGES, z.shape[-1])

def reference(img_feat, txt_feat, img_proj, txt_proj, logit_scale, bias):
    u_img = jnp.dot(img_feat, img_proj, preferred_element_type=jnp.float32)
    u_txt = jnp.dot(txt_feat, txt_proj, preferred_element_type=jnp.float32)
    zf_img, r_img, z_img = normalize(u_img)
    zf_txt, r_txt, z_txt = normalize(u_txt)
    scale = jnp.exp(logit_scale)
    width = GROUP * ROWS
    index = jnp.arange(width)
    sign = jnp.where(index[:, None] == index[None, :], 1.0, -1.0).astype(jnp.float32)

    def one_group(pair):
        left, right = pair
        sims = jnp.dot(left, right.T, preferred_element_type=jnp.float32)
        logit = scale * sims + bias
        loss = jnp.sum(jax.nn.softplus(-sign * logit)) / width
        grads = -sign * jax.nn.sigmoid(-sign * logit) / width
        gsum = jnp.sum(grads)
        gscale = jnp.sum(grads * scale * sims)
        gb = grads.astype(jnp.bfloat16)
        dz_img = scale * jnp.dot(gb, right, preferred_element_type=jnp.float32)
        dz_txt = scale * jnp.dot(gb.T, left, preferred_element_type=jnp.float32)
        return (dz_img, dz_txt, loss, gsum, gscale)
    dz_img, dz_txt, losses, gsums, gscales = lax.map(one_group, (regroup(z_img), regroup(z_txt)))
    dz_img = ungroup(dz_img)
    dz_txt = ungroup(dz_txt)

    def back(dz, zf, r):
        return (r * (dz - zf * lax.optimization_barrier(jnp.sum(zf * dz, axis=1, keepdims=True)))).astype(jnp.bfloat16)
    du_img = back(dz_img, zf_img, r_img)
    du_txt = back(dz_txt, zf_txt, r_txt)
    grad_img = jnp.dot(img_feat.T, du_img, preferred_element_type=jnp.float32)
    grad_txt = jnp.dot(txt_feat.T, du_txt, preferred_element_type=jnp.float32)
    mean_loss = jnp.sum(losses) / IMAGES
    grad_scale = jnp.sum(gscales) / IMAGES
    grad_bias = jnp.sum(gsums) / IMAGES
    return (mean_loss, grad_scale, grad_bias, grad_img, grad_txt)
```

```python
import functools

import jax
import jax.numpy as jnp
from jax import lax
from jax.experimental import pallas as pl
from jax.experimental.pallas import tpu as pltpu
from jax.sharding import PartitionSpec as P

MESH = pl.DeviceIdType.MESH
BF, F32 = jnp.bfloat16, jnp.float32
TXT, IMG = 0, 1
NC = 2
TR = 256


def kernel(dims, ls_ref, bias_ref, imgf, txtf, wi, wt, out_txt, out_img, out_s,
           w, zt, zi, zf, rr, d_t, d_i, st, rt, si, ri, sz, rz,
           p, r0, sx, rx, bb, cz, cy, oo, acc, s0, s1, s2, s3, send, recv):
    rows, embed, shard, width, images = dims
    feats = (txtf, imgf)
    b, m = lax.axis_index("batch"), lax.axis_index("mp")
    xh, z, y = b % 2, (b // 2) % 8, b // 16
    xl, c = m // 2, m % 2
    x = xh * 2 + xl

    def at(xx, yy, zz, cc):
        return ((yy * 8 + zz) * 2 + xx // 2, (xx % 2) * 2 + cc)

    partner = at(x, y, z, 1 - c)
    xs = [at((x + k) % 4, y, z, c) for k in (1, 2, 3)]
    zs = [at(x, y, (z + k) % 8, c) for k in range(1, 8)]
    ys = [at(x, (y + k) % 4, z, c) for k in (1, 2, 3)]
    x2 = xs[1]
    z1 = at(x, y, z + 1 - 2 * (z % 2), c)
    z2 = at(x, y, z + 2 - 4 * ((z // 2) % 2), c)

    barrier = pltpu.get_barrier_semaphore()
    peers = [partner] + xs + zs + ys
    for peer in peers:
        pl.semaphore_signal(barrier, inc=1, device_id=peer, device_id_type=MESH)
    pl.semaphore_wait(barrier, len(peers))

    started = []

    def post(src, dst, peer):
        n = len(started)
        copy = pltpu.make_async_remote_copy(
            src_ref=src, dst_ref=dst, send_sem=send.at[n], recv_sem=recv.at[n],
            device_id=peer, device_id_type=MESH)
        started.append(copy)
        copy.start()
        return copy

    def part(start, size, multiple):
        return pl.ds(pl.multiple_of(start, multiple), size)

    half = shard // 2
    ws = (wt, wi)
    own = [None, None]
    for k in (TXT, IMG):
        mine = m * shard
        own[k] = (
            post(ws[k].at[pl.ds(0, half)], w.at[k, part(mine, half, 16)], xs[0]),
            post(ws[k].at[pl.ds(half, half)], w.at[k, part(mine + half, half, 16)], xs[2]),
            post(ws[k], w.at[k, part(mine, shard, 16)], partner),
        )
    for k in (TXT, IMG):
        w[k, part(m * shard, shard, 16), :] = ws[k][...]
    across = ((1 - xl) * 2 + c) * shard
    passed = [None, None]
    for k in (TXT, IMG):
        own[k][0].wait_recv()
        own[k][1].wait_recv()
        there = w.at[k, part(across, shard, 16)]
        passed[k] = post(there, there, partner)

    acc[...] = jnp.zeros_like(acc)
    scale = jnp.exp(jnp.full((1, embed), ls_ref[0], F32))
    bias = bias_ref[0]
    cr = rows // NC

    def project(k, zall, sends):
        own[k][2].wait_recv()
        passed[k].wait_recv()
        for q in range(NC):
            here = pl.ds(q * cr, cr)
            u = jnp.dot(feats[k][here, :], w[k], preferred_element_type=F32)
            r = lax.rsqrt(jnp.sum(u * u, axis=1, keepdims=True) + 1e-06)
            v = u * r
            zf[k, here, :] = v
            rr[k, here, :] = jnp.broadcast_to(r, (cr, 128))
            zall[0, here, :] = v.astype(BF)
            sends(q, here)

    t_z, t_x, i_z, t_d = [], [], [], []

    def send_txt(q, here):
        t_z.append(post(zt.at[0, here], zt.at[1, here], z1))
        t_x.append(post(zt.at[0, here], zt.at[2, here], x2))

    def send_img(q, here):
        i_z.append(post(zi.at[0, here], zi.at[1, here], z2))

    project(TXT, zt, send_txt)
    project(IMG, zi, send_img)

    def pairs(i, t):
        first_i, first_t = t == 0, i == 0

        def tile(n, carry):
            here = part(n * TR, TR, TR)
            left = zi[i, here, :]
            s = lax.dot_general(left, zt[t], (((1,), (1,)), ((), ())), preferred_element_type=F32)
            logit = scale[:, :rows] * s + bias
            if i == 0 and t == 0:
                row_ids = lax.broadcasted_iota(jnp.int32, s.shape, 0) + n * TR
                col_ids = lax.broadcasted_iota(jnp.int32, s.shape, 1)
                pair = row_ids == col_ids
                logit = jnp.where(pair, -logit, logit)
            e = jnp.exp(-jnp.abs(logit))
            inv = 1.0 / (1.0 + e)
            term = jnp.maximum(logit, 0.0) + jnp.log1p(e)
            g = jnp.where(logit >= 0.0, inv, e * inv)
            if i == 0 and t == 0:
                g = jnp.where(pair, -g, g)
            g = g * (1.0 / width)
            acc[0:1, :] += jnp.sum(term, axis=0, keepdims=True)
            acc[1:2, :] += jnp.sum(g, axis=0, keepdims=True)
            acc[2:3, :] += jnp.sum(g * s, axis=0, keepdims=True)
            gb = g.astype(BF)
            to_i = jnp.dot(gb, zt[t], preferred_element_type=F32)
            to_t = lax.dot_general(gb, left, (((0,), (0,)), ((), ())), preferred_element_type=F32)
            if first_i:
                d_i[i, here, :] = to_i
            else:
                d_i[i, here, :] += to_i
            if first_t:
                @pl.when(n == 0)
                def _():
                    d_t[t] = to_t

                @pl.when(n > 0)
                def _():
                    d_t[t] += to_t
            else:
                d_t[t] += to_t
            return carry

        lax.fori_loop(0, rows // TR, tile, 0)

    pairs(0, 0)
    for q in range(NC):
        here = pl.ds(q * cr, cr)
        t_z[q].wait_recv()
        t_d.append(post(zt.at[1, here], zt.at[3, here], x2))
    pairs(0, 1)
    for q in range(NC):
        t_x[q].wait_recv()
    pairs(0, 2)
    for q in range(NC):
        i_z[q].wait_recv()
    pairs(1, 0)
    pairs(1, 2)
    b_x = [[], []]
    for q in range(NC):
        here = pl.ds(q * cr, cr)
        st[0, here, :] = d_t[2, here, :].astype(BF)
        b_x[0].append(post(st.at[0, here], rt.at[0, here], x2))
    pairs(1, 1)
    for q in range(NC):
        t_d[q].wait_recv()
    pairs(0, 3)
    pairs(1, 3)
    b_i, b_z = [], []
    for q in range(NC):
        here = pl.ds(q * cr, cr)
        st[1, here, :] = d_t[3, here, :].astype(BF)
        b_x[1].append(post(st.at[1, here], rt.at[1, here], x2))
        si[here, :] = d_i[1, here, :].astype(BF)
        b_i.append(post(si.at[here], ri.at[here], z2))
    row = acc[...]
    s0[0] = row[:, 0:128] + row[:, 128:256] + row[:, 256:384] + row[:, 384:512]

    def back(k, dz):
        v, r = zf[k], rr[k][:, 0:1]
        dz = scale * dz
        du = (r * (dz - v * jnp.sum(v * dz, axis=1, keepdims=True))).astype(BF)
        p[k] = lax.dot_general(feats[k][...], du, (((0,), (0,)), ((), ())), preferred_element_type=F32)

    def core_send(k):
        return [post(p.at[k, part((2 * h + 1 - c) * shard, shard, 8)], r0.at[k, h], partner) for h in (0, 1)]

    def x_send(k, arrived):
        for a in arrived:
            a.wait_recv()
        copies = []
        for n in range(3):
            xx = (x + n + 1) % 4
            lo, hi = xx % 2, xx // 2
            sx[k, n] = (p[k, part((2 * lo + c) * shard + hi * half, half, 8), :]
                        + r0[k, lo, part(hi * half, half, 8), :]).astype(sx.dtype)
            copies.append(post(sx.at[k, n], rx.at[k, n], xs[n]))
        bb[k] = p[k, part(m * shard + xh * half, half, 8), :] + r0[k, xl, part(xh * half, half, 8), :]
        return copies

    zr, zc = half // 4, embed // 2

    def corner(zz):
        return part((zz // 2) * zr, zr, 8), part((zz % 2) * zc, zc, 128)

    def z_send(k, arrived):
        for a in arrived:
            a.wait_recv()
        bb[k] = bb[k] + (rx[k, 0].astype(F32) + rx[k, 1].astype(F32) + rx[k, 2].astype(F32))
        copies = []
        for n in range(7):
            i, j = corner((z + n + 1) % 8)
            copies.append(post(bb.at[k, i, j], cz.at[k, n], zs[n]))
        return copies

    def y_send(k, arrived):
        for a in arrived:
            a.wait_recv()
        i, j = corner(z)
        total = bb[k, i, j]
        for n in range(7):
            total = total + cz[k, n]
        cy[k, y] = total
        return [post(cy.at[k, y], cy.at[k, y], ys[n]) for n in range(3)]

    def z_gather(k, arrived):
        for a in arrived:
            a.wait_recv()
        i, j = corner(z)
        i = part(xh * half + (z // 2) * zr, zr, 8)
        oo[k, i, j] = (cy[k, 0] + cy[k, 1]) + (cy[k, 2] + cy[k, 3])
        here = oo.at[k, i, j]
        return [post(here, here, zs[n]) for n in range(7)]

    def x_gather(k, arrived):
        for a in arrived:
            a.wait_recv()
        here = oo.at[k, part(xh * half, half, 8)]
        return [post(here, here, x2)]

    a_s = [post(s0.at[0], s0.at[1], partner)]

    for q in range(NC):
        here = pl.ds(q * cr, cr)
        b_x[1][q].wait_recv()
        sz[here, :] = (d_t[1, here, :] + rt[1, here, :].astype(F32)).astype(BF)
        b_z.append(post(sz.at[here], rz.at[here], z1))
    for q in range(NC):
        b_i[q].wait_recv()
    back(IMG, d_i[0] + ri[...].astype(F32))
    a_i = core_send(IMG)
    a_s[0].wait_recv()
    s1[x] = s0[0] + s0[1]
    a_s = [post(s1.at[x], s1.at[x], peer) for peer in xs]
    a_i = x_send(IMG, a_i)
    for q in range(NC):
        b_x[0][q].wait_recv()
        b_z[q].wait_recv()
    back(TXT, d_t[0] + rt[0].astype(F32) + rz[...].astype(F32))
    a_t = core_send(TXT)
    a_t = x_send(TXT, a_t)
    a_i = z_send(IMG, a_i)
    for a in a_s:
        a.wait_recv()
    s2[z] = (s1[0] + s1[1]) + (s1[2] + s1[3])
    a_s = [post(s2.at[z], s2.at[z], peer) for peer in zs]
    a_t = z_send(TXT, a_t)
    a_i = y_send(IMG, a_i)
    for a in a_s:
        a.wait_recv()
    total = s2[0]
    for n in range(1, 8):
        total = total + s2[n]
    s3[y] = total
    a_s = [post(s3.at[y], s3.at[y], peer) for peer in ys]
    a_t = y_send(TXT, a_t)
    a_i = z_gather(IMG, a_i)
    a_t = z_gather(TXT, a_t)
    a_i = x_gather(IMG, a_i)
    a_t = x_gather(TXT, a_t)
    for a in a_s:
        a.wait_recv()
    total = jnp.sum((s3[0] + s3[1]) + (s3[2] + s3[3]), axis=1, keepdims=True) * (1.0 / images)
    kind = lax.broadcasted_iota(jnp.int32, (8, 128), 0)
    total = jnp.broadcast_to(total, (8, 128))
    total = jnp.where(kind == 0, total * (1.0 / width), total)
    out_s[...] = jnp.where(kind == 2, total * scale[:, 0:128], total)
    a_i[0].wait_recv()
    out_img[...] = oo[IMG]
    a_t[0].wait_recv()
    out_txt[...] = oo[TXT]
    for copy in started:
        copy.wait_send()


def per_device(img_feat, txt_feat, img_proj, txt_proj, logit_scale, bias):
    rows, embed = img_feat.shape
    shard = img_proj.shape[0]
    width = rows * 8
    images = rows * lax.axis_size("batch") * lax.axis_size("mp")
    half = shard // 2
    ar = F32
    v = pltpu.VMEM
    scratch = [
        v((2, embed, embed), BF),
        v((4, rows, embed), BF), v((2, rows, embed), BF),
        v((2, rows, embed), F32), v((2, rows, 128), F32),
        v((4, rows, embed), F32), v((2, rows, embed), F32),
        v((2, rows, embed), BF), v((2, rows, embed), BF),
        v((rows, embed), BF), v((rows, embed), BF),
        v((rows, embed), BF), v((rows, embed), BF),
        v((2, embed, embed), F32), v((2, 2, shard, embed), F32),
        v((2, 3, half, embed), ar), v((2, 3, half, embed), ar),
        v((2, half, embed), F32), v((2, 7, half // 4, embed // 2), F32),
        v((2, 4, half // 4, embed // 2), F32), v((2, shard, embed), F32),
        v((8, rows), F32),
        v((2, 8, 128), F32), v((4, 8, 128), F32), v((8, 8, 128), F32), v((4, 8, 128), F32),
        pltpu.SemaphoreType.DMA((96,)), pltpu.SemaphoreType.DMA((96,)),
    ]
    vm = pl.BlockSpec(memory_space=pltpu.VMEM)
    sm = pl.BlockSpec(memory_space=pltpu.SMEM)
    g_txt, g_img, s = pl.pallas_call(
        functools.partial(kernel, (rows, embed, shard, width, images)),
        out_shape=(
            jax.ShapeDtypeStruct((shard, embed), F32),
            jax.ShapeDtypeStruct((shard, embed), F32),
            jax.ShapeDtypeStruct((8, 128), F32),
        ),
        in_specs=[sm, sm, vm, vm, vm, vm],
        out_specs=(vm, vm, vm),
        scratch_shapes=scratch,
        compiler_params=pltpu.CompilerParams(
            collective_id=0, has_side_effects=True, vmem_limit_bytes=64 * 1024 * 1024 - 65536),
    )(logit_scale.reshape(1), bias.reshape(1), img_feat, txt_feat, img_proj, txt_proj)
    return s[0, 0], s[2, 0], s[1, 0], g_img, g_txt


def solution(mesh):
    return jax.shard_map(
        per_device,
        mesh=mesh,
        in_specs=(
            P(("batch", "mp"), None),
            P(("batch", "mp"), None),
            P("mp", None),
            P("mp", None),
            P(),
            P(),
        ),
        out_specs=(P(), P(), P(), P("mp", None), P("mp", None)),
        check_vma=False,
    )
```

```python
import functools

import jax
import jax.numpy as jnp
from jax import lax
from jax.experimental import pallas as pl
from jax.experimental.pallas import tpu as pltpu
from jax.sharding import PartitionSpec as P

MESH = pl.DeviceIdType.MESH
BF, F32 = jnp.bfloat16, jnp.float32
TXT, IMG = 0, 1


def kernel(dims, ls_ref, bias_ref, imgf, txtf, wi, wt, out_txt, out_img, out_s,
           w, ft, zt, zi, zf, rr, d_t, d_i, st, rt, si, ri, sz, rz,
           p, r0, sx, rx, bb, r2, zb, cz, acc, s0, s1, s2, s3, send, recv):
    rows, embed, shard, width, images = dims
    feats = (txtf, imgf)
    outs = (out_txt, out_img)
    b, m = lax.axis_index("batch"), lax.axis_index("mp")
    xh, z, y = b % 2, (b // 2) % 8, b // 16
    xl, c = m // 2, m % 2
    x = xh * 2 + xl

    def at(xx, yy, zz, cc):
        return ((yy * 8 + zz) * 2 + xx // 2, (xx % 2) * 2 + cc)

    partner = at(x, y, z, 1 - c)
    xs = [at((x + k) % 4, y, z, c) for k in (1, 2, 3)]
    zs = [at(x, y, (z + k) % 8, c) for k in range(1, 8)]
    ys = [at(x, (y + k) % 4, z, c) for k in (1, 2, 3)]
    x2 = xs[1]
    z1 = at(x, y, z + 1 - 2 * (z % 2), c)
    z2 = at(x, y, z + 2 - 4 * ((z // 2) % 2), c)

    barrier = pltpu.get_barrier_semaphore()
    peers = [partner] + xs + zs + ys
    for peer in peers:
        pl.semaphore_signal(barrier, inc=1, device_id=peer, device_id_type=MESH)
    for k in (TXT, IMG):
        ft[k] = feats[k][...].T
    acc[...] = jnp.zeros_like(acc)
    d_i[...] = jnp.zeros_like(d_i)
    d_t[...] = jnp.zeros_like(d_t)
    pl.semaphore_wait(barrier, len(peers))

    started = []

    def post(src, dst, peer):
        n = len(started)
        copy = pltpu.make_async_remote_copy(
            src_ref=src, dst_ref=dst, send_sem=send.at[n], recv_sem=recv.at[n],
            device_id=peer, device_id_type=MESH)
        started.append(copy)
        copy.start()
        return copy

    def part(start, size, multiple):
        return pl.ds(pl.multiple_of(start, multiple), size)

    def wait(copies):
        for copy in copies:
            copy.wait_recv()

    half = shard // 2
    ws = (wt, wi)
    own = [None, None]
    mine = m * shard
    for k in (TXT, IMG):
        own[k] = (
            post(ws[k].at[pl.ds(0, half)], w.at[k, part(mine, half, 16)], xs[0]),
            post(ws[k].at[pl.ds(half, half)], w.at[k, part(mine + half, half, 16)], xs[2]),
            post(ws[k], w.at[k, part(mine, shard, 16)], partner),
        )
    for k in (TXT, IMG):
        w[k, part(mine, shard, 16), :] = ws[k][...]
    scale = jnp.exp(jnp.full((1, embed), ls_ref[0], F32))
    bias = bias_ref[0]
    across = ((1 - xl) * 2 + c) * shard
    CR = rows // 2

    def fetch(k):
        wait(own[k][:2])
        there = w.at[k, part(across, shard, 16)]
        return post(there, there, partner)

    def project(k, passed, zall, sends):
        wait([own[k][2], passed])
        for q in range(2):
            here = pl.ds(q * CR, CR)
            u = jnp.dot(feats[k][here, :], w[k], preferred_element_type=F32)
            r = lax.rsqrt(jnp.sum(u * u, axis=1, keepdims=True) + 1e-06)
            v = u * r
            zf[k, here, :] = v
            rr[k, here, :] = jnp.broadcast_to(r, (CR, 128))
            zall[here, :] = v.astype(BF)
            sends(here)

    def unit(n, q=0):
        return pl.ds(n * rows + q * CR, CR)

    t_z, t_x, i_z, t_d = [], [], [], []
    fine = CR // 2

    def small(n, q):
        return pl.ds(n * rows + q * fine, fine)

    def next_txt():
        q = len(t_z)
        t_z.append(post(zt.at[small(0, q)], zt.at[small(1, q)], z2))

    def next_img():
        q = len(i_z)
        i_z.append(post(zi.at[small(0, q)], zi.at[small(1, q)], z1))

    def send_txt(here):
        q = len(t_x)
        if q == 0:
            next_txt()
            next_txt()
        t_x.append(post(zt.at[here], zt.at[unit(2, q)], x2))

    passed_t = fetch(TXT)
    project(TXT, passed_t, zt, send_txt)
    passed_i = fetch(IMG)
    project(IMG, passed_i, zi, lambda here: None)
    next_img()
    next_txt()
    next_img()
    next_txt()
    next_img()
    next_img()

    def fold(a):
        return jnp.sum(a.reshape(a.shape[0] // 8, 8, a.shape[1]), axis=0)

    def tile(i0, ni, t0, nt, own_pairs=False):
        hi, ht = part(i0, ni, CR), part(t0, nt, CR)
        left, right = zi[hi, :], zt[ht, :]
        s = lax.dot_general(left, right, (((1,), (1,)), ((), ())), preferred_element_type=F32)
        logit = scale[:, :nt] * s + bias
        if own_pairs:
            row_ids = lax.broadcasted_iota(jnp.int32, s.shape, 0) + i0
            col_ids = lax.broadcasted_iota(jnp.int32, s.shape, 1) + t0
            pair = row_ids == col_ids
            logit = jnp.where(pair, -logit, logit)
        e = jnp.exp(logit)
        more = 1.0 + e
        g = e / (more * width)
        if own_pairs:
            g = jnp.where(pair, -g, g)
        term = fold(jnp.log(more[: ni // 2] * more[ni // 2:]))
        gsum, gs = fold(g), fold(g * s)
        for n in range(nt // CR):
            cols = slice(n * CR, n * CR + CR)
            acc[0] += term[:, cols]
            acc[1] += gsum[:, cols]
            acc[2] += gs[:, cols]
        gb = g.astype(BF)
        d_i[hi, :] += jnp.dot(gb, right, preferred_element_type=F32)
        d_t[ht, :] += lax.dot_general(gb, left, (((0,), (0,)), ((), ())), preferred_element_type=F32)

    def loop(count, body):
        def step(n, carry):
            body(n)
            return carry

        lax.fori_loop(0, count, step, 0)

    def relay(q):
        wait(t_z[2 * q:2 * q + 2])
        t_d.append(post(zt.at[unit(1, q)], zt.at[unit(3, q)], x2))

    loop(2, lambda n: tile(n * CR, CR, 0, rows, True))
    relay(0)
    wait(t_x)
    loop(2, lambda n: tile(n * CR, CR, 2 * rows, rows))
    relay(1)
    loop(2, lambda n: tile(n * CR, CR, rows, rows))
    wait(i_z[:2])
    loop(3, lambda n: tile(rows, CR, n * rows, rows))
    wait([t_d[0]])
    loop(3, lambda n: tile(n * CR, CR, 3 * rows, CR))
    wait(i_z[2:])
    tile(rows + CR, CR, 2 * rows, rows)
    b_2, b_3, b_i, b_z = [], [], [], []

    def send_2(q):
        here = pl.ds(q * CR, CR)
        st[here, :] = d_t[unit(2, q), :].astype(BF)
        b_2.append(post(st.at[here], rt.at[here], x2))

    def send_3(q):
        for n in (2 * q, 2 * q + 1):
            here = pl.ds(rows + n * fine, fine)
            st[here, :] = d_t[small(3, n), :].astype(BF)
            b_3.append(post(st.at[here], rt.at[here], x2))

    def send_i(q):
        here = pl.ds(q * fine, fine)
        si[here, :] = d_i[small(1, q), :].astype(BF)
        b_i.append(post(si.at[here], ri.at[here], z1))

    send_2(0)
    tile(rows + CR, CR, 3 * rows, CR)
    send_3(0)
    loop(2, lambda n: tile(rows + CR, CR, n * rows, rows))
    wait([t_d[1]])
    loop(4, lambda n: tile(n * CR, CR, 3 * rows + CR, CR))
    send_3(1)
    send_2(1)
    for q in range(4):
        send_i(q)
    s0[0] = acc[:, :, 0:128] + acc[:, :, 128:256]
    a_s = [post(s0.at[0], s0.at[1], partner)]

    hc = embed // 2
    zr = half // 4

    def back(k, dz):
        v, r = zf[k], rr[k][:, 0:1]
        dz = scale * dz
        du = (r * (dz - v * jnp.sum(v * dz, axis=1, keepdims=True))).astype(BF)
        copies = []
        for j in (0, 1):
            cols = pl.ds(j * hc, hc)
            p[k, :, cols] = lax.dot_general(
                ft[k], du[:, j * hc:(j + 1) * hc], (((1,), (0,)), ((), ())), preferred_element_type=F32)
            copies.append([
                post(p.at[k, part((2 * h + 1 - c) * shard, shard, 8), cols], r0.at[k, h, :, cols], partner)
                for h in (0, 1)])
        return copies

    def block(k, j, yy, xx):
        cols = pl.ds(j * hc, hc)
        if j == 0:
            q = shard // 4
            return jnp.concatenate([
                p[k, part((2 * h + c) * shard + yy * q, q, 8), cols] + r0[k, h, part(yy * q, q, 8), cols]
                for h in (0, 1)], axis=0)
        lo, hi = xx % 2, xx // 2
        return (p[k, part((2 * lo + c) * shard + hi * half, half, 8), cols]
                + r0[k, lo, part(hi * half, half, 8), cols])

    def first(k, j, arrived):
        wait(arrived)
        copies = []
        for n in range(3):
            sx[k, j, n] = block(k, j, (y + n + 1) % 4, (x + n + 1) % 4)
            copies.append(post(sx.at[k, j, n], rx.at[k, j, n], (ys, xs)[j][n]))
        bb[k, j] = block(k, j, y, x)
        return copies

    def second(k, j, arrived):
        wait(arrived)
        bb[k, j] = bb[k, j] + (rx[k, j, 0] + rx[k, j, 1] + rx[k, j, 2])
        copies = []
        for n in range(3):
            xx, yy = (x + n + 1) % 4, (y + n + 1) % 4
            at_row = (xx % 2) * (2 * zr) + (xx // 2) * zr if j == 0 else yy * zr
            copies.append(post(bb.at[k, j, part(at_row, zr, 8)], r2.at[k, j, n], (xs, ys)[j][n]))
        return copies

    mine_z, place = z % 2, (y * (2 * zr) + xh * zr, xh * half + y * zr)

    def third(k, arrived):
        for j in (0, 1):
            wait(arrived[j])
            at_row = xl * (2 * zr) + xh * zr if j == 0 else y * zr
            zb[k, j] = bb[k, j, part(at_row, zr, 8), :] + (r2[k, j, 0] + r2[k, j, 1] + r2[k, j, 2])
        return [post(zb.at[k, 1 - mine_z], zb.at[k, 2], z1)]

    def fourth(k, arrived):
        wait(arrived)
        cz[k, z // 2] = zb[k, mine_z] + zb[k, 2]
        here = cz.at[k, z // 2]
        return [post(here, here, zs[n]) for n in (1, 3, 5)]

    def fifth(k, arrived):
        wait(arrived)
        at_row = (1 - mine_z) * place[0] + mine_z * place[1]
        rows_, cols = part(at_row, zr, 8), part(mine_z * hc, hc, 128)
        outs[k][rows_, cols] = (cz[k, 0] + cz[k, 1]) + (cz[k, 2] + cz[k, 3])
        here = outs[k].at[rows_, cols]
        return [post(here, here, z1)]

    def sixth(k, arrived):
        wait(arrived)
        copies = []
        for j in (0, 1):
            here = outs[k].at[part(place[j], zr, 8), pl.ds(j * hc, hc)]
            copies.append([post(here, here, peer) for peer in ((x2,), ys)[j]])
        return copies

    def seventh(k, j, arrived):
        wait(arrived)
        cols = pl.ds(j * hc, hc)
        here = outs[k].at[part(y * 2 * zr, 2 * zr, 8) if j == 0 else part(xh * half, half, 8), cols]
        return [post(here, here, peer) for peer in (ys, (x2,))[j]]

    def both(stage, k, arrived):
        return [stage(k, j, arrived[j]) for j in (0, 1)]

    for q in range(4):
        here, there = pl.ds(q * fine, fine), pl.ds(rows + q * fine, fine)
        b_3[q].wait_recv()
        sz[here, :] = (d_t[there, :] + rt[there, :].astype(F32)).astype(BF)
        b_z.append(post(sz.at[here], rz.at[here], z2))
    wait(a_s)
    s1[x] = s0[0] + s0[1]
    a_s = [post(s1.at[x], s1.at[x], peer) for peer in xs]
    wait(b_i)
    a_i = back(IMG, d_i[pl.ds(0, rows), :] + ri[...].astype(F32))
    wait(a_s)
    s2[z] = (s1[0] + s1[1]) + (s1[2] + s1[3])
    a_s = [post(s2.at[z], s2.at[z], peer) for peer in zs]
    a_i = both(first, IMG, a_i)
    a_i = both(second, IMG, a_i)
    wait(a_s)
    total = s2[0]
    for n in range(1, 8):
        total = total + s2[n]
    s3[y] = total
    a_s = [post(s3.at[y], s3.at[y], peer) for peer in ys]
    wait(b_2)
    wait(b_z)
    a_t = back(TXT, d_t[pl.ds(0, rows), :] + rt[pl.ds(0, rows), :].astype(F32) + rz[...].astype(F32))
    a_i = third(IMG, a_i)
    a_t = both(first, TXT, a_t)
    a_i = fourth(IMG, a_i)
    a_t = both(second, TXT, a_t)
    a_i = fifth(IMG, a_i)
    a_t = third(TXT, a_t)
    a_i = sixth(IMG, a_i)
    a_t = fourth(TXT, a_t)
    a_i = both(seventh, IMG, a_i)
    a_t = fifth(TXT, a_t)
    a_t = sixth(TXT, a_t)
    a_t = both(seventh, TXT, a_t)
    wait(a_s)
    kinds = (s3[0] + s3[1]) + (s3[2] + s3[3])
    for n, factor in enumerate((1.0 / (images * width), 1.0 / images, 1.0 / images)):
        value = jnp.sum(jnp.sum(kinds[n], axis=1, keepdims=True), axis=0, keepdims=True) * factor
        if n == 2:
            value = value * scale[:, 0:1]
        out_s[n:n + 1, :] = jnp.broadcast_to(value, (1, 128))
    for a in a_i + a_t:
        wait(a)
    for copy in started:
        copy.wait_send()


def per_device(img_feat, txt_feat, img_proj, txt_proj, logit_scale, bias):
    rows, embed = img_feat.shape
    shard = img_proj.shape[0]
    width = rows * 8
    images = rows * lax.axis_size("batch") * lax.axis_size("mp")
    half, hc = shard // 2, embed // 2
    v = pltpu.VMEM
    scratch = [
        v((2, embed, embed), BF), v((2, embed, rows), BF),
        v((4 * rows, embed), BF), v((2 * rows, embed), BF),
        v((2, rows, embed), F32), v((2, rows, 128), F32),
        v((4 * rows, embed), F32), v((2 * rows, embed), F32),
        v((2 * rows, embed), BF), v((2 * rows, embed), BF),
        v((rows, embed), BF), v((rows, embed), BF),
        v((rows, embed), BF), v((rows, embed), BF),
        v((2, embed, embed), F32), v((2, 2, shard, embed), F32),
        v((2, 2, 3, half, hc), F32), v((2, 2, 3, half, hc), F32), v((2, 2, half, hc), F32),
        v((2, 2, 3, half // 4, hc), F32), v((2, 3, half // 4, hc), F32), v((2, 4, half // 4, hc), F32),
        v((3, 8, rows // 2), F32),
        v((2, 3, 8, 128), F32), v((4, 3, 8, 128), F32), v((8, 3, 8, 128), F32), v((4, 3, 8, 128), F32),
        pltpu.SemaphoreType.DMA((128,)), pltpu.SemaphoreType.DMA((128,)),
    ]
    vm = pl.BlockSpec(memory_space=pltpu.VMEM)
    sm = pl.BlockSpec(memory_space=pltpu.SMEM)
    g_txt, g_img, s = pl.pallas_call(
        functools.partial(kernel, (rows, embed, shard, width, images)),
        out_shape=(
            jax.ShapeDtypeStruct((shard, embed), F32),
            jax.ShapeDtypeStruct((shard, embed), F32),
            jax.ShapeDtypeStruct((8, 128), F32),
        ),
        in_specs=[sm, sm, vm, vm, vm, vm],
        out_specs=(vm, vm, vm),
        scratch_shapes=scratch,
        compiler_params=pltpu.CompilerParams(
            collective_id=0, has_side_effects=True, vmem_limit_bytes=64 * 1024 * 1024 - 65536),
    )(logit_scale.reshape(1), bias.reshape(1), img_feat, txt_feat, img_proj, txt_proj)
    return s[0, 0], s[2, 0], s[1, 0], g_img, g_txt


def solution(mesh):
    return jax.shard_map(
        per_device,
        mesh=mesh,
        in_specs=(
            P(("batch", "mp"), None),
            P(("batch", "mp"), None),
            P("mp", None),
            P("mp", None),
            P(),
            P(),
        ),
        out_specs=(P(), P(), P(), P("mp", None), P("mp", None)),
        check_vma=False,
    )
```

```python
import functools

import jax
import jax.numpy as jnp
from jax import lax
from jax.experimental import pallas as pl
from jax.experimental.pallas import tpu as pltpu
from jax.sharding import PartitionSpec as P

MESH = pl.DeviceIdType.MESH
BF, F32 = jnp.bfloat16, jnp.float32
TXT, IMG = 0, 1


def kernel(dims, ls_ref, bias_ref, imgf, txtf, wi, wt, out,
           w, ft, zt, zi, zf, rr, d_t, d_i, st, rt, si, ri, sz, rz,
           p, r0, sx, rx, bb, r2, zb, cz, acc, s0, s1, s2, s3, send, recv):
    rows, embed, shard, width, images = dims
    feats = (txtf, imgf)
    b, m = lax.axis_index("batch"), lax.axis_index("mp")
    xh, z, y = b % 2, (b // 2) % 8, b // 16
    xl, c = m // 2, m % 2
    x = xh * 2 + xl

    def at(xx, yy, zz, cc):
        return ((yy * 8 + zz) * 2 + xx // 2, (xx % 2) * 2 + cc)

    partner = at(x, y, z, 1 - c)
    xs = [at((x + k) % 4, y, z, c) for k in (1, 2, 3)]
    zs = [at(x, y, (z + k) % 8, c) for k in range(1, 8)]
    ys = [at(x, (y + k) % 4, z, c) for k in (1, 2, 3)]
    x2 = xs[1]
    z1 = at(x, y, z + 1 - 2 * (z % 2), c)
    z2 = at(x, y, z + 2 - 4 * ((z // 2) % 2), c)

    barrier = pltpu.get_barrier_semaphore()
    peers = [partner] + xs + zs + ys
    for peer in peers:
        pl.semaphore_signal(barrier, inc=1, device_id=peer, device_id_type=MESH)
    for k in (TXT, IMG):
        ft[k] = feats[k][...].T
    acc[...] = jnp.zeros_like(acc)
    d_i[...] = jnp.zeros_like(d_i)
    d_t[...] = jnp.zeros_like(d_t)
    pl.semaphore_wait(barrier, len(peers))

    started = []

    def post(src, dst, peer):
        n = len(started)
        copy = pltpu.make_async_remote_copy(
            src_ref=src, dst_ref=dst, send_sem=send.at[n], recv_sem=recv.at[n],
            device_id=peer, device_id_type=MESH)
        started.append(copy)
        copy.start()
        return copy

    def part(start, size, multiple):
        return pl.ds(pl.multiple_of(start, multiple), size)

    def wait(copies):
        for copy in copies:
            copy.wait_recv()

    half = shard // 2
    ws = (wt, wi)
    own = [None, None]
    mine = m * shard
    for k in (TXT, IMG):
        own[k] = (
            post(ws[k].at[pl.ds(0, half)], w.at[k, part(mine, half, 16)], xs[0]),
            post(ws[k].at[pl.ds(half, half)], w.at[k, part(mine + half, half, 16)], xs[2]),
        )
    own[TXT] += (post(ws[TXT], w.at[TXT, part(mine, shard, 16)], partner),)
    for k in (TXT, IMG):
        w[k, part(mine, shard, 16), :] = ws[k][...]
    scale = jnp.exp(jnp.full((1, embed), ls_ref[0], F32))
    bias = bias_ref[0]
    across = ((1 - xl) * 2 + c) * shard
    CR = rows // 2

    def fetch(k):
        wait(own[k][:2])
        there = w.at[k, part(across, shard, 16)]
        return post(there, there, partner)

    def project(k, passed, zall, sends):
        wait([own[k][2], passed])
        for q in range(2):
            here = pl.ds(q * CR, CR)
            u = jnp.dot(feats[k][here, :], w[k], preferred_element_type=F32)
            r = lax.rsqrt(jnp.sum(u * u, axis=1, keepdims=True) + 1e-06)
            v = u * r
            zf[k, here, :] = v
            rr[k, here, :] = jnp.broadcast_to(r, (CR, 128))
            zall[here, :] = v.astype(BF)
            sends(here)

    def unit(n, q=0):
        return pl.ds(n * rows + q * CR, CR)

    t_z, t_x, i_z, t_d = [], [], [], []
    fine = CR // 2

    def small(n, q):
        return pl.ds(n * rows + q * fine, fine)

    def next_txt():
        q = len(t_z)
        t_z.append(post(zt.at[small(0, q)], zt.at[small(1, q)], z2))

    def next_img():
        q = len(i_z)
        i_z.append(post(zi.at[small(0, q)], zi.at[small(1, q)], z1))

    def send_txt(here):
        q = len(t_x)
        if q == 0:
            next_txt()
            next_txt()
        t_x.append(post(zt.at[here], zt.at[unit(2, q)], x2))

    passed_t = fetch(TXT)
    project(TXT, passed_t, zt, send_txt)
    own[IMG] += (post(ws[IMG], w.at[IMG, part(mine, shard, 16)], partner),)
    passed_i = fetch(IMG)
    project(IMG, passed_i, zi, lambda here: None)
    next_img()
    next_txt()
    next_img()
    next_txt()
    next_img()
    next_img()

    def fold(a):
        return jnp.sum(a.reshape(a.shape[0] // 8, 8, a.shape[1]), axis=0)

    def tile(i0, ni, t0, nt, own_pairs=False):
        hi, ht = part(i0, ni, CR), part(t0, nt, CR)
        left, right = zi[hi, :], zt[ht, :]
        s = lax.dot_general(left, right, (((1,), (1,)), ((), ())), preferred_element_type=F32)
        logit = scale[:, :nt] * s + bias
        if own_pairs:
            row_ids = lax.broadcasted_iota(jnp.int32, s.shape, 0) + i0
            col_ids = lax.broadcasted_iota(jnp.int32, s.shape, 1) + t0
            pair = row_ids == col_ids
            logit = jnp.where(pair, -logit, logit)
        e = jnp.exp(logit)
        more = 1.0 + e
        g = e / (more * width)
        if own_pairs:
            g = jnp.where(pair, -g, g)
        term = fold(jnp.log(more[: ni // 2] * more[ni // 2:]))
        gsum, gs = fold(g), fold(g * s)
        for n in range(nt // CR):
            cols = slice(n * CR, n * CR + CR)
            acc[0] += term[:, cols]
            acc[1] += gsum[:, cols]
            acc[2] += gs[:, cols]
        gb = g.astype(BF)
        d_i[hi, :] += jnp.dot(gb, right, preferred_element_type=F32)
        d_t[ht, :] += lax.dot_general(gb, left, (((0,), (0,)), ((), ())), preferred_element_type=F32)

    def loop(count, body):
        def step(n, carry):
            body(n)
            return carry

        lax.fori_loop(0, count, step, 0)

    def relay(q):
        wait(t_z[q:q + 1])
        t_d.append(post(zt.at[small(1, q)], zt.at[small(3, q)], x2))

    loop(2, lambda n: tile(n * CR, CR, 0, rows, True))
    relay(0)
    relay(1)
    wait(t_x)
    relay(2)
    loop(2, lambda n: tile(n * CR, CR, 2 * rows, rows))
    relay(3)
    loop(2, lambda n: tile(n * CR, CR, rows, rows))
    wait(i_z[:2])
    loop(3, lambda n: tile(rows, CR, n * rows, rows))
    wait(t_d[:2])
    loop(3, lambda n: tile(n * CR, CR, 3 * rows, CR))
    wait(i_z[2:])
    b_2, b_3, b_i, b_z = [], [], [], []

    def send_2(q):
        here = pl.ds(q * CR, CR)
        st[here, :] = d_t[unit(2, q), :].astype(BF)
        b_2.append(post(st.at[here], rt.at[here], x2))

    def send_3(q):
        for n in (2 * q, 2 * q + 1):
            here = pl.ds(rows + n * fine, fine)
            st[here, :] = d_t[small(3, n), :].astype(BF)
            b_3.append(post(st.at[here], rt.at[here], x2))

    def send_i(q):
        here = pl.ds(q * fine, fine)
        si[here, :] = d_i[small(1, q), :].astype(BF)
        b_i.append(post(si.at[here], ri.at[here], z1))

    tile(rows + CR, CR, 3 * rows, CR)
    send_3(0)
    loop(3, lambda n: tile(rows + CR, CR, n * rows, rows))

    def pass_on(q):
        here, there = pl.ds(q * fine, fine), pl.ds(rows + q * fine, fine)
        b_3[q].wait_recv()
        sz[here, :] = (d_t[there, :] + rt[there, :].astype(F32)).astype(BF)
        b_z.append(post(sz.at[here], rz.at[here], z2))

    wait(t_d[2:])
    loop(2, lambda n: tile(n * CR, CR, 3 * rows + CR, CR))
    pass_on(0)
    loop(2, lambda n: tile(rows + n * CR, CR, 3 * rows + CR, CR))
    send_3(1)
    send_2(0)
    send_2(1)
    send_i(0)
    pass_on(1)
    for q in (1, 2, 3):
        send_i(q)
    s0[0] = acc[:, :, 0:128] + acc[:, :, 128:256]
    a_s = [post(s0.at[0], s0.at[1], partner)]

    hc = embed // 2
    zr = half // 4

    def back(k, dz):
        v, r = zf[k], rr[k][:, 0:1]
        dz = scale * dz
        du = (r * (dz - v * jnp.sum(v * dz, axis=1, keepdims=True))).astype(BF)
        copies = []
        for j in (0, 1):
            cols = pl.ds(j * hc, hc)
            p[k, :, cols] = lax.dot_general(
                ft[k], du[:, j * hc:(j + 1) * hc], (((1,), (0,)), ((), ())), preferred_element_type=F32)
            copies.append([
                post(p.at[k, part((2 * h + 1 - c) * shard, shard, 8), cols], r0.at[k, h, :, cols], partner)
                for h in (0, 1)])
        return copies

    def block(k, j, yy, xx):
        cols = pl.ds(j * hc, hc)
        if j == 0:
            q = shard // 4
            return jnp.concatenate([
                p[k, part((2 * h + c) * shard + yy * q, q, 8), cols] + r0[k, h, part(yy * q, q, 8), cols]
                for h in (0, 1)], axis=0)
        lo, hi = xx % 2, xx // 2
        return (p[k, part((2 * lo + c) * shard + hi * half, half, 8), cols]
                + r0[k, lo, part(hi * half, half, 8), cols])

    def first(k, j, arrived):
        wait(arrived)
        copies = []
        for n in (1, 0, 2):
            sx[k, j, n] = block(k, j, (y + n + 1) % 4, (x + n + 1) % 4)
            copies.append(post(sx.at[k, j, n], rx.at[k, j, n], (ys, xs)[j][n]))
        bb[k, j] = block(k, j, y, x)
        return copies

    def second(k, j, arrived):
        wait(arrived)
        bb[k, j] = bb[k, j] + (rx[k, j, 0] + rx[k, j, 1] + rx[k, j, 2])
        copies = []
        for n in (1, 0, 2):
            xx, yy = (x + n + 1) % 4, (y + n + 1) % 4
            at_row = (xx % 2) * (2 * zr) + (xx // 2) * zr if j == 0 else yy * zr
            copies.append(post(bb.at[k, j, part(at_row, zr, 8)], r2.at[k, j, n], (xs, ys)[j][n]))
        return copies

    mine_z = z % 2

    def third(k, arrived):
        for j in (0, 1):
            wait(arrived[j])
            at_row = xl * (2 * zr) + xh * zr if j == 0 else y * zr
            zb[k, j] = bb[k, j, part(at_row, zr, 8), :] + (r2[k, j, 0] + r2[k, j, 1] + r2[k, j, 2])
        return [post(zb.at[k, 1 - mine_z], zb.at[k, 2], z1)]

    def fourth(k, arrived):
        wait(arrived)
        cz[k, z // 2] = zb[k, mine_z] + zb[k, 2]
        here = cz.at[k, z // 2]
        return [post(here, here, zs[n]) for n in (3, 1, 5)]

    def chunk(k, j, yy, hi):
        at_row = (1 - j) * (yy * (2 * zr) + hi * zr) + j * (hi * half + yy * zr)
        return out.at[part((1 - k) * shard + at_row, zr, 8), part(j * hc, hc, 128)]

    around = (ys[1], x2, ys[0], ys[2])

    def fifth(k, arrived):
        wait(arrived)
        here = chunk(k, mine_z, y, xh)
        here[...] = (cz[k, 0] + cz[k, 1]) + (cz[k, 2] + cz[k, 3])
        return [post(here, here, z1)], [post(here, here, peer) for peer in around]

    def sixth(k, arrived):
        wait(arrived[0])
        here = chunk(k, 1 - mine_z, y, xh)
        return arrived[1], [post(here, here, peer) for peer in around]

    def spread(k, j, arrived):
        wait(arrived)
        copies = []
        for n in (1, 0, 2):
            here = chunk(k, j, (y + j * (n + 1)) % 4, (xh + 1 - j) % 2)
            peer = tuple((1 - j) * a + j * d for a, d in zip(ys[n], x2))
            copies.append(post(here, here, peer))
        return copies

    def seventh(k, arrived):
        return spread(k, mine_z, arrived[0]), arrived[1]

    def eighth(k, arrived):
        return [arrived[0], spread(k, 1 - mine_z, arrived[1])]

    def both(stage, k, arrived):
        return [stage(k, j, arrived[j]) for j in (0, 1)]

    pass_on(2)
    pass_on(3)
    wait(a_s)
    s1[x] = s0[0] + s0[1]
    a_s = [post(s1.at[x], s1.at[x], peer) for peer in xs]
    wait(b_i)
    a_i = back(IMG, d_i[pl.ds(0, rows), :] + ri[...].astype(F32))
    wait(a_s)
    s2[z] = (s1[0] + s1[1]) + (s1[2] + s1[3])
    a_s = [post(s2.at[z], s2.at[z], peer) for peer in zs]
    a_i = both(first, IMG, a_i)
    a_i = both(second, IMG, a_i)
    wait(a_s)
    total = s2[0]
    for n in range(1, 8):
        total = total + s2[n]
    s3[y] = total
    a_s = [post(s3.at[y], s3.at[y], peer) for peer in ys]
    wait(b_2)
    wait(b_z)
    a_t = back(TXT, d_t[pl.ds(0, rows), :] + rt[pl.ds(0, rows), :].astype(F32) + rz[...].astype(F32))
    a_i = third(IMG, a_i)
    a_t = both(first, TXT, a_t)
    a_i = fourth(IMG, a_i)
    a_t = both(second, TXT, a_t)
    a_i = fifth(IMG, a_i)
    a_t = third(TXT, a_t)
    a_i = sixth(IMG, a_i)
    a_t = fourth(TXT, a_t)
    a_i = seventh(IMG, a_i)
    a_i = eighth(IMG, a_i)
    a_t = fifth(TXT, a_t)
    a_t = sixth(TXT, a_t)
    a_t = seventh(TXT, a_t)
    a_t = eighth(TXT, a_t)
    wait(a_s)
    kinds = (s3[0] + s3[1]) + (s3[2] + s3[3])
    for n, factor in enumerate((1.0 / (images * width), 1.0 / images, 1.0 / images)):
        value = jnp.sum(jnp.sum(kinds[n], axis=1, keepdims=True), axis=0, keepdims=True) * factor
        if n == 2:
            value = value * scale[:, 0:1]
        out[2 * shard + n:2 * shard + n + 1, 0:128] = jnp.broadcast_to(value, (1, 128))
    for a in a_i + a_t:
        wait(a)
    for copy in started:
        copy.wait_send()


def per_device(img_feat, txt_feat, img_proj, txt_proj, logit_scale, bias):
    rows, embed = img_feat.shape
    shard = img_proj.shape[0]
    width = rows * 8
    images = rows * lax.axis_size("batch") * lax.axis_size("mp")
    half, hc = shard // 2, embed // 2
    v = pltpu.VMEM
    scratch = [
        v((2, embed, embed), BF), v((2, embed, rows), BF),
        v((4 * rows, embed), BF), v((2 * rows, embed), BF),
        v((2, rows, embed), F32), v((2, rows, 128), F32),
        v((4 * rows, embed), F32), v((2 * rows, embed), F32),
        v((2 * rows, embed), BF), v((2 * rows, embed), BF),
        v((rows, embed), BF), v((rows, embed), BF),
        v((rows, embed), BF), v((rows, embed), BF),
        v((2, embed, embed), F32), v((2, 2, shard, embed), F32),
        v((2, 2, 3, half, hc), F32), v((2, 2, 3, half, hc), F32), v((2, 2, half, hc), F32),
        v((2, 2, 3, half // 4, hc), F32), v((2, 3, half // 4, hc), F32), v((2, 4, half // 4, hc), F32),
        v((3, 8, rows // 2), F32),
        v((2, 3, 8, 128), F32), v((4, 3, 8, 128), F32), v((8, 3, 8, 128), F32), v((4, 3, 8, 128), F32),
        pltpu.SemaphoreType.DMA((128,)), pltpu.SemaphoreType.DMA((128,)),
    ]
    vm = pl.BlockSpec(memory_space=pltpu.VMEM)
    sm = pl.BlockSpec(memory_space=pltpu.SMEM)
    g = pl.pallas_call(
        functools.partial(kernel, (rows, embed, shard, width, images)),
        out_shape=jax.ShapeDtypeStruct((2 * shard + 8, embed), F32),
        in_specs=[sm, sm, vm, vm, vm, vm],
        out_specs=vm,
        scratch_shapes=scratch,
        compiler_params=pltpu.CompilerParams(
            collective_id=0, has_side_effects=True, vmem_limit_bytes=64 * 1024 * 1024 - 65536),
    )(logit_scale.reshape(1), bias.reshape(1), img_feat, txt_feat, img_proj, txt_proj)
    s = g[2 * shard:]
    return s[0, 0], s[2, 0], s[1, 0], g[:shard], g[shard:2 * shard]


def solution(mesh):
    return jax.shard_map(
        per_device,
        mesh=mesh,
        in_specs=(
            P(("batch", "mp"), None),
            P(("batch", "mp"), None),
            P("mp", None),
            P("mp", None),
            P(),
            P(),
        ),
        out_specs=(P(), P(), P(), P("mp", None), P("mp", None)),
        check_vma=False,
    )
```

```python
import functools

import jax
import jax.numpy as jnp
from jax import lax
from jax.experimental import pallas as pl
from jax.experimental.pallas import tpu as pltpu
from jax.sharding import PartitionSpec as P

MESH = pl.DeviceIdType.MESH
BF, F32 = jnp.bfloat16, jnp.float32
TXT, IMG = 0, 1


def kernel(dims, ls_ref, bias_ref, imgf, txtf, wi, wt, out,
           w, ft, zt, zi, zf, rr, d_t, d_i, st, rt, si, ri, sz, rz,
           p, r0, sx, rx, bb, r2, zb, cz, acc, s0, s1, s2, s3, send, recv):
    rows, embed, shard, width, images = dims
    feats = (txtf, imgf)
    b, m = lax.axis_index("batch"), lax.axis_index("mp")
    xh, z, y = b % 2, (b // 2) % 8, b // 16
    xl, c = m // 2, m % 2
    x = xh * 2 + xl

    def at(xx, yy, zz, cc):
        return ((yy * 8 + zz) * 2 + xx // 2, (xx % 2) * 2 + cc)

    partner = at(x, y, z, 1 - c)
    xs = [at((x + k) % 4, y, z, c) for k in (1, 2, 3)]
    zs = [at(x, y, (z + k) % 8, c) for k in range(1, 8)]
    ys = [at(x, (y + k) % 4, z, c) for k in (1, 2, 3)]
    x2 = xs[1]
    z1 = at(x, y, z + 1 - 2 * (z % 2), c)
    z2 = at(x, y, z + 2 - 4 * ((z // 2) % 2), c)

    barrier = pltpu.get_barrier_semaphore()
    peers = [partner] + xs + zs + ys
    for peer in peers:
        pl.semaphore_signal(barrier, inc=1, device_id=peer, device_id_type=MESH)
    for k in (TXT, IMG):
        ft[k] = feats[k][...].T
    acc[...] = jnp.zeros_like(acc)
    d_i[...] = jnp.zeros_like(d_i)
    d_t[...] = jnp.zeros_like(d_t)
    pl.semaphore_wait(barrier, len(peers))

    started = []

    def post(src, dst, peer):
        n = len(started)
        copy = pltpu.make_async_remote_copy(
            src_ref=src, dst_ref=dst, send_sem=send.at[n], recv_sem=recv.at[n],
            device_id=peer, device_id_type=MESH)
        started.append(copy)
        copy.start()
        return copy

    def part(start, size, multiple):
        return pl.ds(pl.multiple_of(start, multiple), size)

    def wait(copies):
        for copy in copies:
            copy.wait_recv()

    half = shard // 2
    ws = (wt, wi)
    own = [None, None]
    mine = m * shard
    for k in (TXT, IMG):
        own[k] = (
            post(ws[k].at[pl.ds(0, half)], w.at[k, part(mine, half, 16)], xs[0]),
            post(ws[k].at[pl.ds(half, half)], w.at[k, part(mine + half, half, 16)], xs[2]),
        )
    own[TXT] += (post(ws[TXT], w.at[TXT, part(mine, shard, 16)], partner),)
    for k in (TXT, IMG):
        w[k, part(mine, shard, 16), :] = ws[k][...]
    scale = jnp.exp(jnp.full((1, embed), ls_ref[0], F32))
    bias = bias_ref[0]
    across = ((1 - xl) * 2 + c) * shard
    CR = rows // 2

    def fetch(k):
        wait(own[k][:2])
        there = w.at[k, part(across, shard, 16)]
        return post(there, there, partner)

    def project(k, passed, zall, sends):
        wait([own[k][2], passed])
        for q in range(2):
            here = pl.ds(q * CR, CR)
            u = jnp.dot(feats[k][here, :], w[k], preferred_element_type=F32)
            r = lax.rsqrt(jnp.sum(u * u, axis=1, keepdims=True) + 1e-06)
            v = u * r
            zf[k, here, :] = v
            rr[k, here, :] = jnp.broadcast_to(r, (CR, 128))
            zall[here, :] = v.astype(BF)
            sends(here)

    def unit(n, q=0):
        return pl.ds(n * rows + q * CR, CR)

    t_z, t_x, i_z, t_d = [], [], [], []
    fine = CR // 2

    def small(n, q):
        return pl.ds(n * rows + q * fine, fine)

    def next_txt():
        q = len(t_z)
        t_z.append(post(zt.at[small(0, q)], zt.at[small(1, q)], z2))

    def next_img():
        q = len(i_z)
        i_z.append(post(zi.at[small(0, q)], zi.at[small(1, q)], z1))

    def send_txt(here):
        q = len(t_x)
        if q == 0:
            next_txt()
            next_txt()
        t_x.append(post(zt.at[here], zt.at[unit(2, q)], x2))

    passed_t = fetch(TXT)
    project(TXT, passed_t, zt, send_txt)
    own[IMG] += (post(ws[IMG], w.at[IMG, part(mine, shard, 16)], partner),)
    passed_i = fetch(IMG)
    project(IMG, passed_i, zi, lambda here: None)
    next_img()
    next_txt()
    next_img()
    next_txt()
    next_img()
    next_img()

    def fold(a):
        return jnp.sum(a.reshape(a.shape[0] // 8, 8, a.shape[1]), axis=0)

    def tile(i0, ni, t0, nt, own_pairs=False):
        hi, ht = part(i0, ni, CR), part(t0, nt, CR)
        left, right = zi[hi, :], zt[ht, :]
        s = lax.dot_general(left, right, (((1,), (1,)), ((), ())), preferred_element_type=F32)
        logit = scale[:, :nt] * s + bias
        if own_pairs:
            row_ids = lax.broadcasted_iota(jnp.int32, s.shape, 0) + i0
            col_ids = lax.broadcasted_iota(jnp.int32, s.shape, 1) + t0
            pair = row_ids == col_ids
            logit = jnp.where(pair, -logit, logit)
        e = jnp.exp(logit)
        more = 1.0 + e
        g = e / (more * width)
        if own_pairs:
            g = jnp.where(pair, -g, g)
        term = fold(jnp.log(more[: ni // 2] * more[ni // 2:]))
        gsum, gs = fold(g), fold(g * s)
        for n in range(nt // CR):
            cols = slice(n * CR, n * CR + CR)
            acc[0] += term[:, cols]
            acc[1] += gsum[:, cols]
            acc[2] += gs[:, cols]
        gb = g.astype(BF)
        d_i[hi, :] += jnp.dot(gb, right, preferred_element_type=F32)
        d_t[ht, :] += lax.dot_general(gb, left, (((0,), (0,)), ((), ())), preferred_element_type=F32)

    def loop(count, body):
        def step(n, carry):
            body(n)
            return carry

        lax.fori_loop(0, count, step, 0)

    def relay(q):
        wait(t_z[q:q + 1])
        t_d.append(post(zt.at[small(1, q)], zt.at[small(3, q)], x2))

    loop(2, lambda n: tile(n * CR, CR, 0, rows, True))
    relay(0)
    relay(1)
    wait(t_x)
    relay(2)
    loop(2, lambda n: tile(n * CR, CR, 2 * rows, rows))
    relay(3)
    loop(2, lambda n: tile(n * CR, CR, rows, rows))
    wait(i_z[:2])
    loop(3, lambda n: tile(rows, CR, n * rows, rows))
    wait(t_d[:2])
    loop(3, lambda n: tile(n * CR, CR, 3 * rows, CR))
    wait(i_z[2:])
    b_2, b_3, b_i, b_z = [], [], [], []

    def send_2(q):
        here = pl.ds(q * CR, CR)
        st[here, :] = d_t[unit(2, q), :].astype(BF)
        b_2.append(post(st.at[here], rt.at[here], x2))

    def send_3(q):
        for n in (2 * q, 2 * q + 1):
            here = pl.ds(rows + n * fine, fine)
            st[here, :] = d_t[small(3, n), :].astype(BF)
            b_3.append(post(st.at[here], rt.at[here], x2))

    def send_i(q):
        here = pl.ds(q * fine, fine)
        si[here, :] = d_i[small(1, q), :].astype(BF)
        b_i.append(post(si.at[here], ri.at[here], z1))

    tile(rows + CR, CR, 3 * rows, CR)
    send_3(0)
    loop(3, lambda n: tile(rows + CR, CR, n * rows, rows))

    def pass_on(q):
        here, there = pl.ds(q * fine, fine), pl.ds(rows + q * fine, fine)
        b_3[q].wait_recv()
        sz[here, :] = (d_t[there, :] + rt[there, :].astype(F32)).astype(BF)
        b_z.append(post(sz.at[here], rz.at[here], z2))

    wait(t_d[2:])
    loop(2, lambda n: tile(n * CR, CR, 3 * rows + CR, CR))
    pass_on(0)
    loop(2, lambda n: tile(rows + n * CR, CR, 3 * rows + CR, CR))
    send_3(1)
    send_2(0)
    send_2(1)
    send_i(0)
    pass_on(1)
    for q in (1, 2, 3):
        send_i(q)
    s0[0] = acc[:, :, 0:128] + acc[:, :, 128:256]
    a_s = [post(s0.at[0], s0.at[1], partner)]

    hc = embed // 2
    zr = half // 4

    def back(k, dz):
        v, r = zf[k], rr[k][:, 0:1]
        dz = scale * dz
        du = (r * (dz - v * jnp.sum(v * dz, axis=1, keepdims=True))).astype(BF)
        copies = []
        for j in (0, 1):
            cols = pl.ds(j * hc, hc)
            p[k, :, cols] = lax.dot_general(
                ft[k], du[:, j * hc:(j + 1) * hc], (((1,), (0,)), ((), ())), preferred_element_type=F32)
            copies.append([
                post(p.at[k, part((2 * h + 1 - c) * shard, shard, 8), cols], r0.at[k, h, :, cols], partner)
                for h in (0, 1)])
        return copies

    def block(k, j, yy, xx):
        cols = pl.ds(j * hc, hc)
        if j == 0:
            q = shard // 4
            return jnp.concatenate([
                p[k, part((2 * h + c) * shard + yy * q, q, 8), cols] + r0[k, h, part(yy * q, q, 8), cols]
                for h in (0, 1)], axis=0)
        lo, hi = xx % 2, xx // 2
        return (p[k, part((2 * lo + c) * shard + hi * half, half, 8), cols]
                + r0[k, lo, part(hi * half, half, 8), cols])

    def first(k, j, arrived):
        wait(arrived)
        copies = []
        for n in (1, 0, 2):
            sx[k, j, n] = block(k, j, (y + n + 1) % 4, (x + n + 1) % 4)
            copies.append(post(sx.at[k, j, n], rx.at[k, j, n], (ys, xs)[j][n]))
        bb[k, j] = block(k, j, y, x)
        return copies

    def second(k, j, arrived):
        wait(arrived)
        bb[k, j] = bb[k, j] + (rx[k, j, 0] + rx[k, j, 1] + rx[k, j, 2])
        copies = []
        for n in (1, 0, 2):
            xx, yy = (x + n + 1) % 4, (y + n + 1) % 4
            at_row = (xx % 2) * (2 * zr) + (xx // 2) * zr if j == 0 else yy * zr
            copies.append(post(bb.at[k, j, part(at_row, zr, 8)], r2.at[k, j, n], (xs, ys)[j][n]))
        return copies

    mine_z = z % 2

    def third(k, arrived):
        for j in (0, 1):
            wait(arrived[j])
            at_row = xl * (2 * zr) + xh * zr if j == 0 else y * zr
            zb[k, j] = bb[k, j, part(at_row, zr, 8), :] + (r2[k, j, 0] + r2[k, j, 1] + r2[k, j, 2])
        return [post(zb.at[k, 1 - mine_z], zb.at[k, 2], z1)]

    def fourth(k, arrived):
        wait(arrived)
        cz[k, z // 2] = zb[k, mine_z] + zb[k, 2]
        here = cz.at[k, z // 2]
        return [post(here, here, zs[n]) for n in (3, 1, 5)]

    def chunk(k, j, yy, hi):
        at_row = (1 - j) * (yy * (2 * zr) + hi * zr) + j * (hi * half + yy * zr)
        return out.at[part((1 - k) * shard + at_row, zr, 8), part(j * hc, hc, 128)]

    around = (ys[1], x2, ys[0], ys[2])

    def fifth(k, arrived):
        wait(arrived)
        here = chunk(k, mine_z, y, xh)
        here[...] = (cz[k, 0] + cz[k, 1]) + (cz[k, 2] + cz[k, 3])
        return [post(here, here, z1)], [post(here, here, peer) for peer in around]

    def sixth(k, arrived):
        wait(arrived[0])
        here = chunk(k, 1 - mine_z, y, xh)
        return arrived[1], [post(here, here, peer) for peer in around]

    def spread(k, j, arrived):
        wait(arrived)
        copies = []
        for n in (1, 0, 2):
            here = chunk(k, j, (y + j * (n + 1)) % 4, (xh + 1 - j) % 2)
            peer = tuple((1 - j) * a + j * d for a, d in zip(ys[n], x2))
            copies.append(post(here, here, peer))
        return copies

    def seventh(k, arrived):
        return spread(k, mine_z, arrived[0]), arrived[1]

    def eighth(k, arrived):
        return [arrived[0], spread(k, 1 - mine_z, arrived[1])]

    def both(stage, k, arrived):
        return [stage(k, j, arrived[j]) for j in (0, 1)]

    pass_on(2)
    pass_on(3)
    wait(a_s)
    s1[x] = s0[0] + s0[1]
    a_s = [post(s1.at[x], s1.at[x], peer) for peer in xs]
    wait(b_i)
    a_i = back(IMG, d_i[pl.ds(0, rows), :] + ri[...].astype(F32))
    wait(a_s)
    s2[z] = (s1[0] + s1[1]) + (s1[2] + s1[3])
    a_s = [post(s2.at[z], s2.at[z], peer) for peer in zs]
    a_i = both(first, IMG, a_i)
    wait(a_s)
    total = s2[0]
    for n in range(1, 8):
        total = total + s2[n]
    s3[y] = total
    a_s = [post(s3.at[y], s3.at[y], peer) for peer in ys]
    wait(b_2)
    wait(b_z)
    a_t = back(TXT, d_t[pl.ds(0, rows), :] + rt[pl.ds(0, rows), :].astype(F32) + rz[...].astype(F32))
    a_i = both(second, IMG, a_i)
    a_t = both(first, TXT, a_t)
    a_i = third(IMG, a_i)
    a_i = fourth(IMG, a_i)
    a_t = both(second, TXT, a_t)
    a_i = fifth(IMG, a_i)
    a_t = third(TXT, a_t)
    a_i = sixth(IMG, a_i)
    a_t = fourth(TXT, a_t)
    a_i = seventh(IMG, a_i)
    a_i = eighth(IMG, a_i)
    a_t = fifth(TXT, a_t)
    a_t = sixth(TXT, a_t)
    a_t = seventh(TXT, a_t)
    a_t = eighth(TXT, a_t)
    wait(a_s)
    kinds = (s3[0] + s3[1]) + (s3[2] + s3[3])
    for n, factor in enumerate((1.0 / (images * width), 1.0 / images, 1.0 / images)):
        value = jnp.sum(jnp.sum(kinds[n], axis=1, keepdims=True), axis=0, keepdims=True) * factor
        if n == 2:
            value = value * scale[:, 0:1]
        out[2 * shard + n:2 * shard + n + 1, 0:128] = jnp.broadcast_to(value, (1, 128))
    for a in a_i + a_t:
        wait(a)
    for copy in started:
        copy.wait_send()


def per_device(img_feat, txt_feat, img_proj, txt_proj, logit_scale, bias):
    rows, embed = img_feat.shape
    shard = img_proj.shape[0]
    width = rows * 8
    images = rows * lax.axis_size("batch") * lax.axis_size("mp")
    half, hc = shard // 2, embed // 2
    v = pltpu.VMEM
    scratch = [
        v((2, embed, embed), BF), v((2, embed, rows), BF),
        v((4 * rows, embed), BF), v((2 * rows, embed), BF),
        v((2, rows, embed), F32), v((2, rows, 128), F32),
        v((4 * rows, embed), F32), v((2 * rows, embed), F32),
        v((2 * rows, embed), BF), v((2 * rows, embed), BF),
        v((rows, embed), BF), v((rows, embed), BF),
        v((rows, embed), BF), v((rows, embed), BF),
        v((2, embed, embed), F32), v((2, 2, shard, embed), F32),
        v((2, 2, 3, half, hc), F32), v((2, 2, 3, half, hc), F32), v((2, 2, half, hc), F32),
        v((2, 2, 3, half // 4, hc), F32), v((2, 3, half // 4, hc), F32), v((2, 4, half // 4, hc), F32),
        v((3, 8, rows // 2), F32),
        v((2, 3, 8, 128), F32), v((4, 3, 8, 128), F32), v((8, 3, 8, 128), F32), v((4, 3, 8, 128), F32),
        pltpu.SemaphoreType.DMA((128,)), pltpu.SemaphoreType.DMA((128,)),
    ]
    vm = pl.BlockSpec(memory_space=pltpu.VMEM)
    sm = pl.BlockSpec(memory_space=pltpu.SMEM)
    g = pl.pallas_call(
        functools.partial(kernel, (rows, embed, shard, width, images)),
        out_shape=jax.ShapeDtypeStruct((2 * shard + 8, embed), F32),
        in_specs=[sm, sm, vm, vm, vm, vm],
        out_specs=vm,
        scratch_shapes=scratch,
        compiler_params=pltpu.CompilerParams(
            collective_id=0, has_side_effects=True, vmem_limit_bytes=64 * 1024 * 1024 - 65536),
    )(logit_scale.reshape(1), bias.reshape(1), img_feat, txt_feat, img_proj, txt_proj)
    s = g[2 * shard:]
    return s[0, 0], s[2, 0], s[1, 0], g[:shard], g[shard:2 * shard]


def solution(mesh):
    return jax.shard_map(
        per_device,
        mesh=mesh,
        in_specs=(
            P(("batch", "mp"), None),
            P(("batch", "mp"), None),
            P("mp", None),
            P("mp", None),
            P(),
            P(),
        ),
        out_specs=(P(), P(), P(), P("mp", None), P("mp", None)),
        check_vma=False,
    )
```
